32 devices in a mesh: fsdp: 8 (over z, x), seq: 4 (over y, core).
Axes of the slice: x: 2, y: 2, z: 4, core: 2. Of those that a mesh axis runs over, the one named last changes fastest.
Arguments:
- inputs: bfloat16 [8, 1024, 768], P('fsdp', 'seq'), may hold values from -6 to 6
- norm1_gain: bfloat16 [768], P('fsdp'), may hold values from 0.5 to 1.5
- norm1_shift: bfloat16 [768], P('fsdp'), may hold values from -3 to 3
- qkv_weight: bfloat16 [768, 2304], P('fsdp'), may hold values from -2 to 2, as said below
- qkv_bias: bfloat16 [2304], P('fsdp'), may hold values from -3 to 3
- out_weight: bfloat16 [768, 768], P('fsdp'), may hold values from -0.875 to 0.875
- out_bias: bfloat16 [768], P('fsdp'), may hold values from -3 to 3
- norm2_gain: bfloat16 [768], P('fsdp'), may hold values from 0.5 to 1.5
- norm2_shift: bfloat16 [768], P('fsdp'), may hold values from -3 to 3
- up_weight: bfloat16 [768, 3072], P('fsdp'), may hold values from -0.21875 to 0.21875
- up_bias: bfloat16 [3072], P('fsdp'), may hold values from -3 to 3
- down_weight: bfloat16 [3072, 768], P('fsdp'), may hold values from -0.109375 to 0.109375
- down_bias: bfloat16 [768], P('fsdp'), may hold values from -3 to 3
- cotangent: bfloat16 [8, 1024, 768], P('fsdp', 'seq'), may hold values from -6 to 6
Outputs:
- output: bfloat16 [8, 1024, 768], P('fsdp', 'seq')
- input_grad: float32 [8, 1024, 768], P('fsdp', 'seq')
- norm1_gain_grad: float32 [768], P('fsdp')
- norm1_shift_grad: float32 [768], P('fsdp')
- qkv_weight_grad: float32 [768, 2304], P('fsdp')
- qkv_bias_grad: float32 [2304], P('fsdp')
- out_weight_grad: float32 [768, 768], P('fsdp')
- out_bias_grad: float32 [768], P('fsdp')
- norm2_gain_grad: float32 [768], P('fsdp')
- norm2_shift_grad: float32 [768], P('fsdp')
- up_weight_grad: float32 [768, 3072], P('fsdp')
- up_bias_grad: float32 [3072], P('fsdp')
- down_weight_grad: float32 [3072, 768], P('fsdp')
- down_bias_grad: float32 [768], P('fsdp')
The draws below stay inside these ranges and needn't reach their ends.
Inputs may be any that keep to these rules, and one draw needn't show every extreme that they name: `qkv_weight`: query, key and value columns of each head in the layout of the steps.
All inputs are finite; a program needn't handle non-finite values.
Results may differ from the reference program's by a relative error of at most 0.012.
The reference program's roundings to bfloat16 on the way count: a program that leaves them out, or rounds other values in their place, can miss the bound.
Values may be sent and summed in bfloat16 or wider, within the bound.
No kernel may reach another device: no remote copies, remote signals or barrier semaphores. Data moves between devices by JAX's collectives and lax.ppermute only.
A program may use at most 128 MiB of HBM per device.

```python
import math
import jax
import jax.numpy as jnp
from jax import lax

D = 768
HEADS = 12
HEAD = 64
ROT = 16
FF = 3072
LENGTH = 1024
SEQUENCES = 8


def draw_qkv_weight(key, part):
    base = jax.random.truncated_normal(key, -4.0, 4.0, (D, HEADS, 3, HEAD), jnp.float32) / math.sqrt(D)
    return base.reshape(D, 3 * D).astype(jnp.bfloat16)


def with_spikes(drawn, own_key, source, target, parts, factor):
    def block_of(axis_at):
        return (jnp.arange(drawn.shape[axis_at]) // (drawn.shape[axis_at] // parts)).reshape((-1,) + (1,) * (drawn.ndim - 1 - axis_at))

    near = jax.random.permutation(own_key, parts)[block_of(target)]
    other_side = (block_of(target) + parts // 2) % parts
    return jnp.where((block_of(source) == near) | (block_of(source) == other_side), factor * drawn, drawn)


def level_of(key, extent, cuts, least, largest):
    factor_of, own = 1.0, jax.random.fold_in(key, 6)
    for axis_at, blocks in cuts:
        steps = jnp.exp(jax.random.uniform(jax.random.fold_in(own, axis_at), (blocks,), jnp.float32, least / len(cuts), largest / len(cuts)))
        factor_of = factor_of * jnp.repeat(steps, extent[axis_at] // blocks).reshape([-1 if axis == axis_at else 1 for axis in range(len(extent))])
    return factor_of


def bell_draw(own_key, extent, spread, bound, pieces=(), held_as=jnp.bfloat16):
    drawn = jax.random.normal(own_key, extent, jnp.float32) * spread
    if len(pieces) > 0:
        drawn = level_of(own_key, extent, pieces, -0.22, 0.18) * drawn
    return jnp.clip(drawn, min=-bound, max=bound).astype(held_as)


def noise_with(stream_key, dims, width, most, split, heavy, dtype=jnp.bfloat16):
    values = width * jax.random.normal(stream_key, dims, jnp.float32)
    if split:
        values = values * level_of(stream_key, dims, split, -0.22, 0.18)
    return jnp.clip(with_spikes(values, jax.random.fold_in(stream_key, 3), *heavy), -most, most).astype(dtype)


def setup_inputs(seed: int = 0) -> dict:
    arg_keys = jax.random.split(jax.random.key(seed), 15)
    inputs = bell_draw(arg_keys[0], (SEQUENCES, LENGTH, D), 1.0, 6.0, ((0, 8), (1, 4)))
    norm1_gain = jnp.clip(1.0 + 0.1 * jax.random.normal(arg_keys[1], (D,), jnp.float32), 0.5, 1.5).astype(jnp.bfloat16)
    norm1_shift = bell_draw(arg_keys[2], (D,), 0.5, 3.0, ((0, 8),))
    qkv_weight = draw_qkv_weight(jax.random.fold_in(arg_keys[14], 71), 0)
    qkv_bias = bell_draw(arg_keys[4], (3 * D,), 0.5, 3.0, ((0, 8),))
    out_weight = bell_draw(arg_keys[5], (D, D), (D // 16) ** -0.5, 0.875, ((0, 8),))
    out_bias = bell_draw(arg_keys[6], (D,), 0.5, 3.0, ((0, 8),))
    norm2_gain = jnp.clip(1.0 + 0.1 * jax.random.normal(arg_keys[7], (D,), jnp.float32), 0.5, 1.5).astype(jnp.bfloat16)
    norm2_shift = bell_draw(arg_keys[8], (D,), 0.5, 3.0, ((0, 8),))
    up_weight = bell_draw(arg_keys[9], (D, FF), D ** -0.5, 0.21875, ((0, 8),))
    up_bias = bell_draw(arg_keys[10], (FF,), 0.5, 3.0, ((0, 8),))
    down_weight = bell_draw(arg_keys[11], (FF, D), FF ** -0.5, 0.109375, ((0, 8),))
    down_bias = bell_draw(arg_keys[12], (D,), 0.5, 3.0, ((0, 8),))
    cotangent = noise_with(arg_keys[13], (SEQUENCES, LENGTH, D), 1.0, 6.0, ((0, 8), (1, 4)), (0, 2, 8, 2.0))
    return dict(inputs=inputs, norm1_gain=norm1_gain, norm1_shift=norm1_shift, qkv_weight=qkv_weight, qkv_bias=qkv_bias, out_weight=out_weight, out_bias=out_bias, norm2_gain=norm2_gain, norm2_shift=norm2_shift, up_weight=up_weight, up_bias=up_bias, down_weight=down_weight, down_bias=down_bias, cotangent=cotangent)


epsilon = 1e-05
root_half = 0.7071067811865476
inv_root_tau = 0.3989422804014327

def norm_forward(values, scales, shifts):
    center = values - lax.optimization_barrier(jnp.mean(values, axis=-1, keepdims=True))
    scale_inv = lax.rsqrt(lax.optimization_barrier(jnp.mean(center * center, axis=-1, keepdims=True)) + epsilon)
    normed = center * scale_inv
    return (normed * scales + shifts, normed, scale_inv)

def norm_backward(grad_rows, normed, scale_inv, scales):
    scaled = grad_rows * scales
    gradient = scale_inv * (scaled - lax.optimization_barrier(jnp.mean(scaled, axis=-1, keepdims=True)) - normed * lax.optimization_barrier(jnp.mean(scaled * normed, axis=-1, keepdims=True)))
    return (gradient, lax.optimization_barrier(jnp.sum(grad_rows * normed, axis=0)), lax.optimization_barrier(jnp.sum(grad_rows, axis=0)))

def rotary_tables(length, rot_dims):
    places = jnp.arange(length).astype(jnp.float32)
    frequency = jnp.exp(jnp.arange(rot_dims // 2).astype(jnp.float32) * (-2.0 * math.log(10000.0) / rot_dims))
    angles = places[:, None] * frequency[None, :]
    cosine_table = jnp.concatenate([jnp.cos(angles), jnp.cos(angles)], axis=1)[:, None, :]
    sine_table = jnp.concatenate([jnp.sin(angles), jnp.sin(angles)], axis=1)[:, None, :]
    return (cosine_table, sine_table)

def rotate(values, cosine_table, sine_table, rot_dims):
    half_dims = rot_dims // 2
    leading = values[..., :rot_dims]
    turned = jnp.concatenate([-leading[..., half_dims:], leading[..., :half_dims]], axis=-1)
    return jnp.concatenate([leading * cosine_table + turned * sine_table, values[..., rot_dims:]], axis=-1)

def unrotate(gradient, cosine_table, sine_table, rot_dims):
    half_dims = rot_dims // 2
    leading = gradient[..., :rot_dims]
    mixed_sine = leading * sine_table
    reverse = jnp.concatenate([mixed_sine[..., half_dims:], -mixed_sine[..., :half_dims]], axis=-1)
    return jnp.concatenate([leading * cosine_table + reverse, gradient[..., rot_dims:]], axis=-1)

def gelu_exact(values):
    return 0.5 * values * (1.0 + lax.erf(values * root_half))

def gelu_slope(values):
    return 0.5 * (1.0 + lax.erf(values * root_half)) + values * jnp.exp(-0.5 * values * values) * inv_root_tau

def masked_scores(q_rot, k_rot):
    score_scale = 1.0 / math.sqrt(HEAD)
    scores = jnp.einsum('qhd,khd->hqk', q_rot.astype(jnp.float32), k_rot.astype(jnp.float32)) * score_scale
    length = q_rot.shape[0]
    allowed = jnp.arange(length)[:, None] >= jnp.arange(length)[None, :]
    return jnp.where(allowed[None], scores, -jnp.inf)

def attend(q_rot, k_rot, values):
    scores = masked_scores(q_rot, k_rot)
    row_max = lax.optimization_barrier(jnp.max(scores, axis=-1, keepdims=True))
    log_total = row_max + jnp.log(lax.optimization_barrier(jnp.sum(jnp.exp(scores - row_max), axis=-1, keepdims=True)))
    probabilities = jnp.exp(scores - log_total).astype(jnp.bfloat16)
    attended = jnp.einsum('hqk,khd->qhd', probabilities.astype(jnp.float32), values.astype(jnp.float32)).astype(jnp.bfloat16)
    return (attended, log_total)

def attend_back(q_rot, k_rot, values, attended, log_total, d_att, cosine_table, sine_table):
    score_scale = 1.0 / math.sqrt(HEAD)
    probabilities = jnp.exp(masked_scores(q_rot, k_rot) - log_total)
    row_dot = lax.optimization_barrier(jnp.sum(d_att.astype(jnp.float32) * attended.astype(jnp.float32), axis=-1))
    d_prob = jnp.einsum('qhd,khd->hqk', d_att.astype(jnp.float32), values.astype(jnp.float32))
    d_scores = (probabilities * (d_prob - row_dot.T[:, :, None]) * score_scale).astype(jnp.bfloat16)
    grad_value = jnp.einsum('hqk,qhd->khd', probabilities.astype(jnp.bfloat16).astype(jnp.float32), d_att.astype(jnp.float32)).astype(jnp.bfloat16)
    grad_query = jnp.einsum('hqk,khd->qhd', d_scores.astype(jnp.float32), k_rot.astype(jnp.float32))
    grad_key = jnp.einsum('hqk,qhd->khd', d_scores.astype(jnp.float32), q_rot.astype(jnp.float32))
    grad_query = unrotate(grad_query, cosine_table, sine_table, ROT).astype(jnp.bfloat16)
    grad_key = unrotate(grad_key, cosine_table, sine_table, ROT).astype(jnp.bfloat16)
    return (grad_query, grad_key, grad_value)

def reference(inputs, norm1_gain, norm1_shift, qkv_weight, qkv_bias, out_weight, out_bias, norm2_gain, norm2_shift, up_weight, up_bias, down_weight, down_bias, cotangent):
    cosine_table, sine_table = rotary_tables(LENGTH, ROT)
    gain_one = norm1_gain.astype(jnp.float32)
    shift_one = norm1_shift.astype(jnp.float32)
    gain_two = norm2_gain.astype(jnp.float32)
    shift_two = norm2_shift.astype(jnp.float32)

    def one_sequence(totals, sliced):
        tokens, cot_rows = sliced
        inputs_wide = tokens.astype(jnp.float32)
        first_wide, first_hat, first_inv = norm_forward(inputs_wide, gain_one, shift_one)
        first_norm = first_wide.astype(jnp.bfloat16)
        qkv_rows = (jnp.dot(first_norm, qkv_weight, preferred_element_type=jnp.float32) + qkv_bias.astype(jnp.float32)).astype(jnp.bfloat16)
        by_head = qkv_rows.reshape(LENGTH, HEADS, 3, HEAD)
        q_rot = rotate(by_head[:, :, 0].astype(jnp.float32), cosine_table, sine_table, ROT).astype(jnp.bfloat16)
        k_rot = rotate(by_head[:, :, 1].astype(jnp.float32), cosine_table, sine_table, ROT).astype(jnp.bfloat16)
        value_heads = by_head[:, :, 2]
        attended, log_total = attend(q_rot, k_rot, value_heads)
        att_rows = attended.reshape(LENGTH, D)
        branch = jnp.dot(att_rows, out_weight, preferred_element_type=jnp.float32) + out_bias.astype(jnp.float32)
        second_wide, second_hat, second_inv = norm_forward(inputs_wide, gain_two, shift_two)
        second_norm = second_wide.astype(jnp.bfloat16)
        pre_act = jnp.dot(second_norm, up_weight, preferred_element_type=jnp.float32) + up_bias.astype(jnp.float32)
        hidden = gelu_exact(pre_act).astype(jnp.bfloat16)
        result = (inputs_wide + branch + jnp.dot(hidden, down_weight, preferred_element_type=jnp.float32) + down_bias.astype(jnp.float32)).astype(jnp.bfloat16)
        cot_wide = cot_rows.astype(jnp.float32)
        bias_sum = lax.optimization_barrier(jnp.sum(cot_wide, axis=0))
        grad_out_w = jnp.dot(att_rows.T, cot_rows, preferred_element_type=jnp.float32)
        grad_down_w = jnp.dot(hidden.T, cot_rows, preferred_element_type=jnp.float32)
        d_pre = (jnp.dot(cot_rows, down_weight.T, preferred_element_type=jnp.float32) * gelu_slope(pre_act)).astype(jnp.bfloat16)
        grad_up_w = jnp.dot(second_norm.T, d_pre, preferred_element_type=jnp.float32)
        grad_up_b = lax.optimization_barrier(jnp.sum(d_pre.astype(jnp.float32), axis=0))
        d_second = jnp.dot(d_pre, up_weight.T, preferred_element_type=jnp.float32)
        d_att = jnp.dot(cot_rows, out_weight.T, preferred_element_type=jnp.float32).astype(jnp.bfloat16).reshape(LENGTH, HEADS, HEAD)
        grad_query, grad_key, grad_value = attend_back(q_rot, k_rot, value_heads, attended, log_total, d_att, cosine_table, sine_table)
        d_qkv = jnp.stack([grad_query, grad_key, grad_value], axis=2).reshape(LENGTH, 3 * D)
        grad_qkv_w = jnp.dot(first_norm.T, d_qkv, preferred_element_type=jnp.float32)
        grad_qkv_b = lax.optimization_barrier(jnp.sum(d_qkv.astype(jnp.float32), axis=0))
        d_first = jnp.dot(d_qkv, qkv_weight.T, preferred_element_type=jnp.float32)
        d_input_one, grad_gain_one, grad_shift_one = norm_backward(d_first, first_hat, first_inv, gain_one)
        d_input_two, grad_gain_two, grad_shift_two = norm_backward(d_second, second_hat, second_inv, gain_two)
        input_grad = cot_wide + d_input_one + d_input_two
        terms = (grad_gain_one, grad_shift_one, grad_qkv_w, grad_qkv_b, grad_out_w, bias_sum, grad_gain_two, grad_shift_two, grad_up_w, grad_up_b, grad_down_w)
        totals = jax.tree.map(lambda before, added: before + added, totals, terms)
        return (totals, (result, input_grad))
    zeros_start = (jnp.zeros((D,), jnp.float32), jnp.zeros((D,), jnp.float32), jnp.zeros((D, 3 * D), jnp.float32), jnp.zeros((3 * D,), jnp.float32), jnp.zeros((D, D), jnp.float32), jnp.zeros((D,), jnp.float32), jnp.zeros((D,), jnp.float32), jnp.zeros((D,), jnp.float32), jnp.zeros((D, FF), jnp.float32), jnp.zeros((FF,), jnp.float32), jnp.zeros((FF, D), jnp.float32))
    totals, stacked = lax.scan(one_sequence, zeros_start, (inputs, cotangent))
    return (stacked[0], stacked[1], totals[0], totals[1], totals[2], totals[3], totals[4], totals[5], totals[6], totals[7], totals[8], totals[9], totals[10], totals[5])
```

```python
import functools
import math

import jax
import jax.numpy as jnp
import numpy as np
from jax import lax
from jax.experimental import pallas as pl
from jax.experimental.pallas import tpu as pltpu
from jax.sharding import PartitionSpec as P

HEADS = 12
HEAD = 64
ROT = 16
RING_MOST = 8
VECTORS = 12
VEC_ROWS = 16
VEC_LANE = 640


epsilon = 1e-05
root_half = 0.7071067811865476
inv_root_tau = 0.3989422804014327

BF = jnp.bfloat16
F32 = jnp.float32
NN = (((1,), (0,)), ((), ()))
NT = (((1,), (1,)), ((), ()))
TN = (((0,), (0,)), ((), ()))
MIB = 1 << 20


def mm(a, b, dims):
    return lax.dot_general(a, b, dims, preferred_element_type=F32)


def ringed(n):
    return n <= RING_MOST and n % 2 == 0


def ring_owners(n):
    order, _ = ring_order(n)
    rows = []
    for rank in range(n):
        p = order.index(rank)
        row = [rank]
        for k in range(1, n // 2):
            row += [order[(p - k) % n], order[(p + k) % n]]
        rows.append(row + [order[(p + n // 2) % n]])
    return np.array(rows, np.int32)


def ring_order(n):
    order = list(range(0, n, 2)) + list(range(n - 1, 0, -2))
    return order, [(order[i], order[(i + 1) % n]) for i in range(n)]


def my_owners(n):
    if not ringed(n):
        return None
    rank = lax.axis_index("fsdp")
    return lax.dynamic_index_in_dim(jnp.asarray(ring_owners(n)), rank, 0, keepdims=False)


def ring_links(n):
    _, right = ring_order(n)
    return right, [(b, a) for a, b in right]


def ring_gather(block):
    n = lax.axis_size("fsdp")
    if not ringed(n):
        return [lax.all_gather(block, "fsdp", axis=0)]
    right, left = ring_links(n)
    half = block.shape[1] // 2
    pieces = [block]
    r = l = block
    for _ in range(1, n // 2):
        r = lax.ppermute(r, "fsdp", right)
        l = lax.ppermute(l, "fsdp", left)
        pieces += [r, l]
    pieces.append(lax.ppermute(r[:, :half], "fsdp", right))
    pieces.append(lax.ppermute(l[:, half:], "fsdp", left))
    return pieces


def swap(values, axis, bit):
    return lax.ppermute(values, axis, [(i, i ^ bit) for i in range(lax.axis_size(axis))])


def small_gather(values):
    bit = 1
    me = lax.axis_index("fsdp")
    while bit < lax.axis_size("fsdp"):
        other = swap(values, "fsdp", bit)
        mine_low = (me & bit) == 0
        values = jnp.concatenate(
            [jnp.where(mine_low, values, other), jnp.where(mine_low, other, values)], axis=0
        )
        bit *= 2
    return values


def transpose_links(n, seq):
    return [(g, (g % n) * seq + g // n) for g in range(n * seq)]


def chunks_of(values):
    core = swap(values, "seq", 1)
    across = swap(values, "seq", 2)
    return [values, core, across, swap(across, "seq", 1)]


def in_vmem():
    return pl.BlockSpec(memory_space=pltpu.VMEM)


def call(kernel, outs, args, scalars=(), scratch=(), flops=0, name=None, limit=16):
    moved = sum(a.size * a.dtype.itemsize for a in args) + sum(
        math.prod(s) * jnp.dtype(d).itemsize for s, d in outs
    )
    return pl.pallas_call(
        kernel,
        out_shape=[jax.ShapeDtypeStruct(s, d) for s, d in outs],
        in_specs=[pl.BlockSpec(memory_space=pltpu.SMEM) for _ in scalars] + [in_vmem() for _ in args],
        out_specs=[in_vmem() for _ in outs],
        scratch_shapes=list(scratch),
        cost_estimate=pl.CostEstimate(flops=flops, bytes_accessed=moved, transcendentals=0),
        compiler_params=pltpu.CompilerParams(vmem_limit_bytes=limit * MIB),
        name=name,
    )(*scalars, *args)


def select_kernel(n, seq, me_ref, up_ref, down_ref, qkv_ref, ff_ref, qkv_out_ref):
    part = up_ref.shape[0]
    rows = down_ref.shape[0] // seq
    sub = up_ref.shape[1] // (n * seq)
    heads = HEADS // seq
    wide = 3 * HEAD
    used = heads * wide
    for m in range(seq):

        @pl.when(me_ref[0] == m)
        def _():
            cuts = [(r * seq + m) * sub for r in range(n)]
            ff_ref[:part, :] = jnp.concatenate([up_ref[:, c : c + sub] for c in cuts], axis=1)
            ff_ref[part:, :] = down_ref[m * rows : (m + 1) * rows, :]
            starts = [m * used + h * wide for h in range(heads)]
            blocks = [qkv_ref[:, c : c + 2 * HEAD] for c in starts]
            blocks += [qkv_ref[:, c + 2 * HEAD : c + wide] for c in starts]
            pad = qkv_out_ref.shape[1] - used
            blocks.append(jnp.zeros((part, pad), BF))
            qkv_out_ref[...] = jnp.concatenate(blocks, axis=1)


def normalize(values):
    center = values - jnp.mean(values, axis=-1, keepdims=True)
    inv = lax.rsqrt(jnp.mean(center * center, axis=-1, keepdims=True) + epsilon)
    return center * inv, inv


def prepare_kernel(me_ref, x0, x1, x2, x3, hat_ref):
    rows = x0.shape[0]
    for k, x_ref in enumerate((x0, x1, x2, x3)):
        at = pl.ds(pl.multiple_of((me_ref[0] ^ k) * rows, rows), rows)
        hat_ref[at, :] = normalize(x_ref[...].astype(F32))[0]


def spread(owners, refs, parts):
    width = refs[0].shape[1]
    half = width // 2
    for i, ref in enumerate(refs):
        owner = owners[min(i, len(refs) - 2)]
        for dest, first, rows, columns in parts:
            at = pl.ds(pl.multiple_of(owner * rows, 8), rows)
            if i < len(refs) - 2:
                dest[at, :] = ref[first : first + rows, :columns]
            elif i == len(refs) - 2:
                dest[at, :half] = ref[first : first + rows, :]
            else:
                dest[at, half:columns] = ref[first : first + rows, : columns - half]


def ffn_kernel(ring, tile, n, *refs):
    if ring:
        me_ref, owners, refs = refs[0], refs[1], refs[2:]
        pieces, refs = refs[:ring], refs[ring:]
        c0, c1, c2, c3, hat_ref, affine, bias = refs[:7]
        part_ref, d_ref, g_ref, gbias, gnorm, cot_ref = refs[7:13]
        up, down, hidden, d_pre, sn = refs[13:]
        rows = pieces[0].shape[0] // 2
        width = up.shape[1]
        spread(owners, pieces, [(up, 0, rows, width), (down, rows, rows, width)])
    else:
        me_ref, up, down, c0, c1, c2, c3, hat_ref, affine, bias = refs[:10]
        part_ref, d_ref, g_ref, gbias, gnorm, cot_ref = refs[10:16]
        hidden, d_pre, sn = refs[16:]
        rows = up.shape[0] // n
    size = c0.shape[0]
    for k, c_ref in enumerate((c0, c1, c2, c3)):
        cot_ref[pl.ds(pl.multiple_of((me_ref[0] ^ k) * size, size), size), :] = c_ref[...]
    gbias[...] = jnp.zeros_like(gbias)
    gnorm[...] = jnp.zeros_like(gnorm)

    def step(t, carry):
        at = pl.ds(pl.multiple_of(t * tile, tile), tile)
        norm = (hat_ref[at, :] * affine[2:3, :] + affine[3:4, :]).astype(BF)
        sn[at, :] = norm
        pre = mm(norm, up[...], NN) + bias[...]
        rise = 0.5 * (1.0 + lax.erf(pre * root_half))
        act = (pre * rise).astype(BF)
        hidden[at, :] = act
        part_ref[at, :] = mm(act, down[...], NN)
        slope = rise + pre * jnp.exp(-0.5 * pre * pre) * inv_root_tau
        d_act = (mm(cot_ref[at, :], down[...], NT) * slope).astype(BF)
        d_pre[at, :] = d_act
        gbias[...] += jnp.sum(d_act.astype(F32), axis=0, keepdims=True)
        d_second = mm(d_act, up[...], NT)
        gnorm[0:1, :] += jnp.sum(d_second * hat_ref[at, :], axis=0, keepdims=True)
        gnorm[1:2, :] += jnp.sum(d_second, axis=0, keepdims=True)
        d_ref[at, :] = d_second * affine[2:3, :]
        return carry

    lax.fori_loop(0, hat_ref.shape[0] // tile, step, 0)
    grad = mm(sn[...], d_pre[...], TN)
    for j in range(n):
        g_ref[j, :rows, :] = grad[j * rows : (j + 1) * rows]
    grad = mm(hidden[...], cot_ref[...], TN)
    for j in range(n):
        g_ref[j, rows:, :] = grad[j * rows : (j + 1) * rows]


def turn(values, table_ref, sign):
    half, wide = ROT // 2, 2 * HEAD
    turned = (
        pltpu.roll(values, wide - half, 1) * table_ref[1]
        + pltpu.roll(values, half, 1) * table_ref[2]
    )
    return values * table_ref[0] + sign * turned


def qkv_kernel(ring, heads, tile, *refs):
    used = heads * 3 * HEAD
    if ring:
        owners, refs = refs[0], refs[1:]
        pieces, refs = refs[:ring], refs[ring:]
        hat_ref, cot_ref, affine, bias, table = refs[:5]
        fn, qk, val, d_att, w, outw = refs[5:]
        part = hat_ref.shape[1] // (ring - 1)
        out_rows = pieces[0].shape[0] - part
        spread(owners, pieces, [(w, 0, part, used), (outw, part, out_rows, hat_ref.shape[1])])
    else:
        w, outw, hat_ref, cot_ref, affine, bias, table = refs[:7]
        fn, qk, val, d_att = refs[7:]
    scale = 1.0 / math.sqrt(HEAD)
    lane = lax.broadcasted_iota(jnp.int32, (1, 2 * HEAD), 1)
    scaling = jnp.where(lane < HEAD, scale, 1.0)

    def step(t, carry):
        at = pl.ds(pl.multiple_of(t * tile, tile), tile)
        norm = (hat_ref[at, :] * affine[0:1, :] + affine[1:2, :]).astype(BF)
        fn[at, :] = norm
        rows = (mm(norm, w[...], NN) + bias[...]).astype(BF)
        for h in range(heads):
            both = rows[:, h * 2 * HEAD : (h + 1) * 2 * HEAD].astype(F32)
            both = turn(both, table.at[:, at, :], 1.0).astype(BF).astype(F32)
            qk[at, h * 2 * HEAD : (h + 1) * 2 * HEAD] = (both * scaling).astype(BF)
        val[at, :] = rows[:, heads * 2 * HEAD :]
        d_att[at, :] = mm(cot_ref[at, :], outw[...], NT).astype(BF)
        return carry

    lax.fori_loop(0, hat_ref.shape[0] // tile, step, 0)


def attend_kernel(head, block, qk_ref, val_ref, datt_ref, table, att_ref, dqk_ref, dv_ref, dkt, dvt):
    length = qk_ref.shape[0]
    both = qk_ref[:, head * 2 * HEAD : (head + 1) * 2 * HEAD]
    q_s, k_r = both[:, :HEAD], both[:, HEAD:]
    val = val_ref[:, head * HEAD : (head + 1) * HEAD]
    d_att = datt_ref[:, head * HEAD : (head + 1) * HEAD]
    scale = 1.0 / math.sqrt(HEAD)
    dkt[...] = jnp.zeros_like(dkt)
    dvt[...] = jnp.zeros_like(dvt)
    allowed = lax.broadcasted_iota(jnp.int32, (block, block), 0) >= lax.broadcasted_iota(
        jnp.int32, (block, block), 1
    )
    d_q = []
    for i in range(length // block):
        lo, hi = i * block, (i + 1) * block
        q_i = q_s[lo:hi]
        da_i = d_att[lo:hi]
        scores = mm(q_i, k_r[:hi], NT)
        diag = jnp.where(allowed, scores[:, lo:hi], -jnp.inf)
        scores = diag if i == 0 else jnp.concatenate([scores[:, :lo], diag], axis=1)
        top = jnp.max(scores, axis=-1, keepdims=True)
        raised = jnp.exp(scores - top)
        probs = raised * (1.0 / jnp.sum(raised, axis=-1, keepdims=True))
        p_b = probs.astype(BF)
        att = mm(p_b, val[:hi], NN).astype(BF)
        att_ref[lo:hi, :] = att
        row_dot = jnp.sum(da_i.astype(F32) * att.astype(F32), axis=-1, keepdims=True)
        d_prob = mm(da_i, val[:hi], NT)
        d_s = (probs * (d_prob - row_dot)).astype(BF)
        d_q.append(mm(d_s, k_r[:hi], NN) * scale)
        dvt[:, :hi] += mm(da_i, p_b, TN)
        dkt[:, :hi] += mm(q_i, d_s, TN)
    for i in range(length // block):
        lo, hi = i * block, (i + 1) * block
        d_both = jnp.concatenate([d_q[i], dkt[:, lo:hi].T], axis=1)
        dqk_ref[lo:hi, :] = turn(d_both, table.at[:, lo:hi, :], -1.0).astype(BF)
        dv_ref[lo:hi, :] = dvt[:, lo:hi].T.astype(BF)


def close_kernel(heads, me_ref, *refs):
    atts, refs = refs[:heads], refs[heads:]
    d_qks, refs = refs[:heads], refs[heads:]
    d_vs, refs = refs[:heads], refs[heads:]
    w, outw, part_ref, d_ref, hat_ref, affine = refs[:6]
    give, keep, gnorm, gbias, d_all, att_all = refs[6:]
    for h in range(heads):
        d_all[:, h * 2 * HEAD : (h + 1) * 2 * HEAD] = d_qks[h][...]
    d_all[:, heads * 2 * HEAD :] = jnp.concatenate([d[...] for d in d_vs], axis=1)
    att_all[...] = jnp.concatenate([a[...] for a in atts], axis=1)
    gnorm[...] = jnp.zeros_like(gnorm)
    gbias[...] = jnp.zeros_like(gbias)
    size = hat_ref.shape[0] // 4
    low = me_ref[0] & 1

    def step(t, carry):
        at = pl.ds(pl.multiple_of(t * size, size), size)
        d_rows = d_all[at, :]
        total = part_ref[at, :] + mm(att_all[at, :], outw[...], NN)
        d_first = mm(d_rows, w[...], NT)
        gbias[...] += jnp.sum(d_rows.astype(F32), axis=0, keepdims=True)
        gnorm[0:1, :] += jnp.sum(d_first * hat_ref[at, :], axis=0, keepdims=True)
        gnorm[1:2, :] += jnp.sum(d_first, axis=0, keepdims=True)
        d_hat = (d_ref[at, :] + d_first * affine[0:1, :]).astype(BF)
        total = total.astype(BF)
        across = t // 2

        @pl.when((t & 1) == low)
        def _():
            keep[0, across] = total
            keep[1, across] = d_hat

        @pl.when((t & 1) != low)
        def _():
            give[0, across] = total
            give[1, across] = d_hat

        return carry

    lax.fori_loop(0, 4, step, 0)


def meet_kernel(me_ref, keep, got, give, mine):
    high = me_ref[0] >> 1
    for kind in range(2):
        give[kind] = (keep[kind, 1 - high].astype(F32) + got[kind, 1 - high].astype(F32)).astype(BF)
        mine[kind] = keep[kind, high].astype(F32) + got[kind, high].astype(F32)


def grads_kernel(n, seq, me_ref, fn, cot, d_all, att_all, gn1, gn2, gbias_qkv, gbias_up, own_cot, g_ref, vec):
    part = fn.shape[1] // n
    used = d_all.shape[1]
    out_rows = att_all.shape[1] // n
    heads = HEADS // seq
    me = me_ref[0]
    grad = mm(fn[...], d_all[...], TN)
    pad = jnp.zeros((part, fn.shape[1] - used), F32)
    for j in range(n):
        g_ref[j, :part, :] = jnp.concatenate([grad[j * part : (j + 1) * part], pad], axis=1)
    grad = mm(att_all[...], cot[...], TN)
    for j in range(n):
        g_ref[j, part:, :] = grad[j * out_rows : (j + 1) * out_rows]
    vec[...] = jnp.zeros_like(vec)
    bias = jnp.sum(own_cot[...].astype(F32), axis=0, keepdims=True)
    wide = jnp.concatenate([gn1[...], gn2[...], bias], axis=0)
    for j in range(n):
        vec[j, 0:5, :] = wide[:, j * part : (j + 1) * part]
    shifts = gbias_qkv[...]
    ordered = []
    for h in range(heads):
        ordered.append(shifts[:, h * 2 * HEAD : (h + 1) * 2 * HEAD])
        ordered.append(shifts[:, heads * 2 * HEAD + h * HEAD : heads * 2 * HEAD + (h + 1) * HEAD])
    ordered = jnp.concatenate(ordered, axis=1)
    for i in range(n // seq):
        for k in range(3):
            c = (3 * i + k) * part
            vec[me * (n // seq) + i, 5 + k : 6 + k, :] = ordered[:, c : c + part]
    rises = gbias_up[...]
    for m in range(seq):

        @pl.when(me == m)
        def _():
            for j in range(n):
                vec[j, 8 + m : 9 + m, :] = rises[:, j * part : (j + 1) * part]


def hop_kernel(stage, with_vec, picks, at_ref, *refs):
    refs = list(refs)
    block_r = refs.pop(0)
    block_l = refs.pop(0) if stage not in (0, 1) else block_r
    vec = refs.pop(0) if with_vec else None
    came_r = refs.pop(0) if stage != 1 else None
    came_l = refs.pop(0) if stage != 1 else None
    width = block_r.shape[2]
    half = width // 2
    spot = slice(VEC_LANE, VEC_LANE + vec.shape[2]) if with_vec else None
    near = slice(VEC_LANE - half, VEC_LANE - half + vec.shape[2]) if with_vec else None

    def vectors(dest, lanes, index, sources):
        total = vec[at_ref[picks[index]]]
        for ref, columns in sources:
            total += ref[:VEC_ROWS, columns].astype(F32)
            total += ref[VEC_ROWS : 2 * VEC_ROWS, columns].astype(F32)
        top = total.astype(BF)
        dest[:VEC_ROWS, lanes] = top
        dest[VEC_ROWS : 2 * VEC_ROWS, lanes] = (total - top.astype(F32)).astype(BF)

    if stage == 1:
        send_r, send_l = refs
        send_r[...] = block_r[0, :, :half].astype(BF)
        send_l[...] = block_r[0, :, half:].astype(BF)
        if with_vec:
            vectors(send_l, near, 0, [])
    elif stage == 2:
        send_r, send_l = refs
        send_r[:, :half] = (block_r[0, :, :half] + came_r[...].astype(F32)).astype(BF)
        send_r[:, half:] = block_r[0, :, half:].astype(BF)
        send_l[:, :half] = block_l[0, :, :half].astype(BF)
        send_l[:, half:] = (block_l[0, :, half:] + came_l[...].astype(F32)).astype(BF)
        if with_vec:
            vectors(send_r, spot, 0, [])
            vectors(send_l, spot, 1, [(came_l, near)])
    elif stage == 3:
        send_r, send_l = refs
        send_r[...] = (block_r[0] + came_r[...].astype(F32)).astype(BF)
        send_l[...] = (block_l[0] + came_l[...].astype(F32)).astype(BF)
        if with_vec:
            vectors(send_r, spot, 0, [(came_r, spot)])
            vectors(send_l, spot, 1, [(came_l, spot)])
    else:
        (out,) = refs
        out[...] = (block_r[0] + came_r[...].astype(F32) + came_l[...].astype(F32)).astype(BF)
        if with_vec:
            vectors(out, spot, 0, [(came_r, spot), (came_l, spot)])


def hop(stage, grads, vec, owners, picks, came, name):
    n, rows, width = grads.shape
    half = width // 2
    pick_r = pl.BlockSpec((1, rows, width), lambda i, at: (at[picks[0]], 0, 0))
    pick_l = pl.BlockSpec((1, rows, width), lambda i, at: (at[picks[1]], 0, 0))
    args, specs = [grads], [pick_r]
    if stage not in (0, 1):
        args.append(grads)
        specs.append(pick_l)
    if vec is not None:
        args.append(vec)
        specs.append(in_vmem())
    args += list(came)
    specs += [in_vmem() for _ in came]
    shape = (rows, half) if stage == 1 else (rows, width)
    count = 1 if stage == 0 else 2
    return pl.pallas_call(
        functools.partial(hop_kernel, stage, vec is not None, picks),
        out_shape=[jax.ShapeDtypeStruct(shape, BF)] * count,
        grid_spec=pltpu.PrefetchScalarGridSpec(
            num_scalar_prefetch=1, grid=(1,), in_specs=specs, out_specs=[in_vmem()] * count
        ),
        cost_estimate=pl.CostEstimate(
            flops=2 * rows * width, bytes_accessed=8 * rows * width, transcendentals=0
        ),
        compiler_params=pltpu.CompilerParams(vmem_limit_bytes=8 * MIB),
        name=name,
    )(owners, *args)


def ring_scatter(grads, vec, owners, name):
    n = lax.axis_size("fsdp")
    if not ringed(n):
        total = lax.psum_scatter(grads, "fsdp", scatter_dimension=0, tiled=True)[0].astype(BF)
        if vec is None:
            return total, None
        return total, lax.psum_scatter(vec, "fsdp", scatter_dimension=0, tiled=True)[0]
    right, left = ring_links(n)
    came = ()
    for t in range(1, n // 2 + 1):
        at = n // 2 - t + 1
        sent = hop(
            min(t, 3),
            grads,
            vec,
            owners,
            (2 * at, 2 * at - 1) if at < n // 2 else (n - 1, n - 1),
            came,
            "%s_hop%d" % (name, t),
        )
        came = (lax.ppermute(sent[0], "fsdp", right), lax.ppermute(sent[1], "fsdp", left))
    return hop(0, grads, vec, owners, (0, 0), came, name + "_own")[0], None


def finish_ffn_kernel(n, me_ref, c0, c1, c2, c3, up_ref, down_ref, held, lower):
    part = up_ref.shape[0]
    rows = down_ref.shape[0] // 4
    me = me_ref[0]
    for k, c in enumerate((c0, c1, c2, c3)):
        a = me ^ k
        held[a] = c[:part, :]
        lower[a] = c[part:, :]
    for a in range(4):
        down_ref[a * rows : (a + 1) * rows, :] = lower[a].astype(F32)
    sub = up_ref.shape[1] // (4 * n)
    pieces = [held[a][:, r * sub : (r + 1) * sub] for r in range(n) for a in range(4)]
    up_ref[...] = jnp.concatenate(pieces, axis=1).astype(F32)


def finish_kernel(part, me_ref, *refs):
    chunks, refs = refs[:4], refs[4:]
    vecs = None
    if len(refs) == 16:
        vecs, refs = refs[:4], refs[4:]
    qkv_ref, out_ref = refs[:2]
    g1, s1, g2, s2, gb, gq, gu = refs[2:9]
    held, small, lower = refs[9:]
    me = me_ref[0]
    rows = out_ref.shape[0] // 4
    used = held.shape[2]
    heads = HEADS // 4
    for k, c in enumerate(chunks):
        a = me ^ k
        held[a] = c[:part, :used]
        lower[a] = c[part:, :]
        if vecs is None:
            lanes = slice(VEC_LANE, VEC_LANE + part)
            small[a] = c[:VEC_ROWS, lanes].astype(F32) + c[VEC_ROWS : 2 * VEC_ROWS, lanes].astype(F32)
        else:
            small[a] = vecs[k][...]
    pieces = []
    for a in range(4):
        out_ref[a * rows : (a + 1) * rows, :] = lower[a].astype(F32)
        rows_a = held[a]
        for h in range(heads):
            pieces.append(rows_a[:, h * 2 * HEAD : (h + 1) * 2 * HEAD])
            pieces.append(rows_a[:, (2 * heads + h) * HEAD : (2 * heads + h + 1) * HEAD])
    qkv_ref[...] = jnp.concatenate(pieces, axis=1).astype(F32)
    total = small[0] + small[1] + small[2] + small[3]
    for i, ref in enumerate((g1, s1, g2, s2, gb)):
        ref[...] = total[i : i + 1, :]
    gq[...] = jnp.concatenate([total[5 + i : 6 + i, :] for i in range(3)], axis=1)
    gu[...] = jnp.concatenate([total[8 + i : 9 + i, :] for i in range(4)], axis=1)


def rotary_tables(length):
    half = ROT // 2
    places = jnp.arange(length).astype(F32)
    lane = jnp.arange(2 * HEAD) % HEAD
    frequency = jnp.exp((lane % half).astype(F32) * (-2.0 * math.log(10000.0) / ROT))
    angles = places[:, None] * frequency[None, :]
    turning = (lane < ROT)[None, :]
    sine = jnp.sin(angles)
    cosine = jnp.where(turning, jnp.cos(angles), 1.0)
    return jnp.stack(
        [
            cosine,
            jnp.where((lane < half)[None, :], -sine, 0.0),
            jnp.where(turning & (lane >= half)[None, :], sine, 0.0),
        ]
    )


def per_device(
    inputs,
    norm1_gain,
    norm1_shift,
    qkv_weight,
    qkv_bias,
    out_weight,
    out_bias,
    norm2_gain,
    norm2_shift,
    up_weight,
    up_bias,
    down_weight,
    down_bias,
    cotangent,
):
    n, seq = lax.axis_size("fsdp"), lax.axis_size("seq")
    me = lax.axis_index("seq")
    seq_count, local_len, width = inputs.shape
    assert seq_count == 1 and seq == 4
    length = local_len * seq
    part = norm1_gain.shape[0]
    heads = HEADS // seq
    hidden_all = up_weight.shape[1]
    units = hidden_all // seq
    used = heads * 3 * HEAD
    down_rows, out_rows = down_weight.shape[0] // seq, out_weight.shape[0] // seq
    swap_links = transpose_links(n, seq)
    back_links = [(b, a) for a, b in swap_links]
    who = me.reshape(1).astype(jnp.int32)

    out_mine = lax.ppermute(
        lax.dynamic_slice_in_dim(out_weight, me * out_rows, out_rows, 0),
        ("fsdp", "seq"),
        swap_links,
    )
    ff_mine, qkv_mine = call(
        functools.partial(select_kernel, n, seq),
        [((part + down_rows, width), BF), ((part, width), BF)],
        [up_weight, down_weight, qkv_weight],
        scalars=[who],
        name="select",
    )
    x_rows = inputs.reshape(local_len, width)
    cot_rows = cotangent.reshape(local_len, width)
    x_chunks = chunks_of(x_rows)
    owners = my_owners(n)
    ff_pieces = ring_gather(ff_mine)

    small = jnp.concatenate(
        [
            v.reshape(-1, part)
            for v in (
                norm1_gain,
                norm1_shift,
                norm2_gain,
                norm2_shift,
                out_bias,
                down_bias,
                qkv_bias,
                up_bias,
            )
        ]
    )[None]
    small = small_gather(small).astype(F32)
    affine = jnp.moveaxis(small[:, :6], 1, 0).reshape(6, width)
    qkv_shift = small[:, 6:9].reshape(3 * width)
    qkv_shift = lax.dynamic_slice_in_dim(qkv_shift, me * used, used, 0).reshape(heads, 3, HEAD)
    qkv_shift = jnp.concatenate(
        [qkv_shift[:, :2].reshape(1, -1), qkv_shift[:, 2].reshape(1, -1)], axis=1
    )
    up_shift = lax.dynamic_index_in_dim(small[:, 9:], me, 1, keepdims=False).reshape(1, units)

    cot_chunks = chunks_of(cot_rows)
    q_pieces = ring_gather(jnp.concatenate([qkv_mine, out_mine], axis=0))

    rows_f = ((length, width), F32)
    rows_b = ((length, width), BF)
    (hat,) = call(prepare_kernel, [rows_f], x_chunks, scalars=[who], name="prepare")
    work = [pltpu.VMEM((length, units), BF), pltpu.VMEM((length, units), BF), pltpu.VMEM((length, width), BF)]
    if owners is None:
        gathered = ff_pieces[0]
        ff_pieces = [
            gathered[:, :part].reshape(width, units),
            gathered[:, part:].reshape(units, width),
        ]
        scalars = [who]
    else:
        scalars = [who, owners]
        work = [pltpu.VMEM((width, units), BF), pltpu.VMEM((units, width), BF)] + work
    part_out, d_two, grad_ff, grad_up_b, grad_norm2, cot = call(
        functools.partial(
            ffn_kernel, 0 if owners is None else len(ff_pieces), length // 4, n
        ),
        [
            rows_f,
            rows_f,
            ((n, part + down_rows, width), F32),
            ((1, units), F32),
            ((2, width), F32),
            rows_b,
        ],
        ff_pieces + cot_chunks + [hat, affine, up_shift],
        scalars=scalars,
        scratch=work,
        flops=12 * length * width * units,
        name="ffn",
        limit=28,
    )
    ff_sum, _ = ring_scatter(grad_ff, None, owners, "ff")

    table = rotary_tables(length)
    outs = [
        rows_b,
        ((length, heads * 2 * HEAD), BF),
        ((length, heads * HEAD), BF),
        ((length, heads * HEAD), BF),
    ]
    if owners is None:
        gathered = q_pieces[0]
        w_all = gathered[:, :part, :used].reshape(width, used)
        out_all = gathered[:, part:].reshape(heads * HEAD, width)
        q_pieces = [w_all, out_all]
    else:
        outs += [((width, used), BF), ((heads * HEAD, width), BF)]
    made = call(
        functools.partial(qkv_kernel, 0 if owners is None else len(q_pieces), heads, length // 4),
        outs,
        q_pieces + [hat, cot, affine, qkv_shift, table],
        scalars=[] if owners is None else [owners],
        flops=2 * length * width * heads * 4 * HEAD,
        name="qkv",
        limit=20,
    )
    first_norm, qk, val, d_att = made[:4]
    if owners is not None:
        w_all, out_all = made[4:]
    atts, d_qks, d_vs = [], [], []
    for h in range(heads):
        att, d_qk, d_v = call(
            functools.partial(attend_kernel, h, length // 4),
            [((length, HEAD), BF), ((length, 2 * HEAD), BF), ((length, HEAD), BF)],
            [qk, val, d_att, table],
            scratch=[pltpu.VMEM((HEAD, length), F32), pltpu.VMEM((HEAD, length), F32)],
            flops=16 * length * length * HEAD,
            name="attend%d" % h,
            limit=16,
        )
        atts.append(att)
        d_qks.append(d_qk)
        d_vs.append(d_v)
    exchange = ((2, 2, local_len, width), BF)
    give, keep, grad_norm1, grad_qkv_b, d_all, att_all = call(
        functools.partial(close_kernel, heads),
        [
            exchange,
            exchange,
            ((2, width), F32),
            ((1, used), F32),
            ((length, used), BF),
            ((length, heads * HEAD), BF),
        ],
        atts + d_qks + d_vs + [w_all, out_all, part_out, d_two, hat, affine],
        scalars=[who],
        flops=2 * length * width * heads * 4 * HEAD,
        name="close",
        limit=20,
    )
    got = swap(give, "seq", 1)
    grad_q, vec = call(
        functools.partial(grads_kernel, n, seq),
        [((n, part + out_rows, width), F32), ((n, VEC_ROWS, part), F32)],
        [first_norm, cot, d_all, att_all, grad_norm1, grad_norm2, grad_qkv_b, grad_up_b, cot_rows],
        scalars=[who],
        flops=2 * length * width * heads * 4 * HEAD,
        name="grads",
        limit=20,
    )
    q_sum, vec_sum = ring_scatter(grad_q, vec, owners, "q")

    give, mine = call(
        meet_kernel,
        [((2, local_len, width), BF), ((2, local_len, width), F32)],
        [keep, got],
        scalars=[who],
        name="meet",
    )
    total = mine + swap(give, "seq", 2).astype(F32)
    x_wide = x_rows.astype(F32)
    cot_wide = cot_rows.astype(F32)
    output = (x_wide + total[0] + affine[4:5] + affine[5:6]).astype(BF)
    d_hat = total[1]
    own_hat, own_inv = normalize(x_wide)
    input_grad = cot_wide + own_inv * (
        d_hat
        - jnp.mean(d_hat, axis=-1, keepdims=True)
        - own_hat * jnp.mean(d_hat * own_hat, axis=-1, keepdims=True)
    )

    up_all, down_all = call(
        functools.partial(finish_ffn_kernel, n),
        [((part, hidden_all), F32), ((down_rows * seq, width), F32)],
        chunks_of(ff_sum),
        scalars=[who],
        scratch=[pltpu.VMEM((seq, part, units), BF), pltpu.VMEM((seq, down_rows, width), BF)],
        name="finish_ffn",
    )
    out_back = lax.ppermute(q_sum[part:], ("fsdp", "seq"), back_links)
    payload = chunks_of(jnp.concatenate([q_sum[:part], out_back], axis=0))
    if vec_sum is not None:
        payload = payload + chunks_of(vec_sum)
    rows_of = [((1, part), F32)] * 5 + [((1, 3 * part), F32), ((1, 4 * part), F32)]
    qkv_g, out_g, g1, s1, g2, s2, gb, gq, gu = call(
        functools.partial(finish_kernel, part),
        [((part, 3 * width), F32), ((out_rows * seq, width), F32)] + rows_of,
        payload,
        scalars=[who],
        scratch=[
            pltpu.VMEM((seq, part, used), BF),
            pltpu.VMEM((seq, VEC_ROWS, part), F32),
            pltpu.VMEM((seq, out_rows, width), BF),
        ],
        name="finish",
    )
    g1, s1, g2, s2, gb, gq, gu = (v.reshape(-1) for v in (g1, s1, g2, s2, gb, gq, gu))
    return (
        output.reshape(inputs.shape),
        input_grad.reshape(inputs.shape),
        g1,
        s1,
        qkv_g,
        gq,
        out_g,
        gb,
        g2,
        s2,
        up_all,
        gu,
        down_all,
        gb,
    )


def solution(mesh):
    row, matrix, tokens = P("fsdp"), P("fsdp", None), P("fsdp", "seq", None)
    return jax.shard_map(
        per_device,
        mesh=mesh,
        in_specs=(
            tokens,
            row,
            row,
            matrix,
            row,
            matrix,
            row,
            row,
            row,
            matrix,
            row,
            matrix,
            row,
            tokens,
        ),
        out_specs=(
            tokens,
            tokens,
            row,
            row,
            matrix,
            row,
            matrix,
            row,
            row,
            row,
            matrix,
            row,
            matrix,
            row,
        ),
        check_vma=False,
    )
```
